32 devices in a mesh: dp: 2 (over core), expert: 16 (over z, y, x).
Axes of the slice: x: 2, y: 2, z: 4, core: 2. Of those that a mesh axis runs over, the one named last changes fastest.
Arguments:
- inputs: bfloat16 [4096, 2048], P(('dp', 'expert')), may hold values from -6 to 6
- out_grad: bfloat16 [4096, 2048], P(('dp', 'expert')), may hold values from -6 to 6
- routes: int32 [4096, 8], P(('dp', 'expert')), may hold values from 0 to 15, all different within a row; in each aligned block of 128 rows (0 to 127, 128 to 255, ...) at most 96 rows name the same one
- combine: float32 [4096, 8], P(('dp', 'expert')), may hold values from 0.05 to 1
- saved_gate: bfloat16 [2, 16, 1536, 768], P('dp', 'expert'), may hold values from -6 to 6
- saved_up: bfloat16 [2, 16, 1536, 768], P('dp', 'expert'), may hold values from -6 to 6
- w_gate: bfloat16 [16, 2048, 768], P('expert', 'dp'), may hold values from -0.125 to 0.125
- w_up: bfloat16 [16, 2048, 768], P('expert', 'dp'), may hold values from -0.125 to 0.125
- w_down: bfloat16 [16, 768, 2048], P('expert', None, 'dp'), may hold values from -0.21875 to 0.21875
Outputs:
- input_grad: bfloat16 [4096, 2048], P(('dp', 'expert'))
- gate_grad: float32 [16, 2048, 768], P('expert', 'dp')
- up_grad: float32 [16, 2048, 768], P('expert', 'dp')
- down_grad: float32 [16, 768, 2048], P('expert', None, 'dp')
The draws below stay inside these ranges and needn't reach their ends.
Inputs may be any that keep to these rules, and one draw needn't show every extreme that they name: `routes`: in the 128 rows of one device, no expert is named by more than 96 choices, a bound that some block reaches.
All inputs are finite; a program needn't handle non-finite values.
Results may differ from the reference program's by a relative error of at most 0.0064.
Values may be sent and summed in bfloat16 or wider, within the bound.
No kernel may reach another device: no remote copies, remote signals or barrier semaphores. Data moves between devices by JAX's collectives and lax.ppermute only.
A program may use at most 192 MiB of HBM per device.

```python
import math
import jax
import jax.numpy as jnp
import numpy as np
from jax import lax

D = 2048
FF = 768
TOP = 8
TOK_DEV = 128
EXPERTS = 16
REPLICAS = 2
TOKENS = 4096
SLOTS = 1536
CAP = 96


def level_of(stream_key, dims, cuts, low, largest):
    def one(dim, parts):
        draws = jax.random.uniform(jax.random.fold_in(jax.random.fold_in(stream_key, 6), dim), (parts,), jnp.float32, low / len(cuts), largest / len(cuts))
        return jnp.repeat(jnp.exp(draws), dims[dim] // parts).reshape((-1,) + (1,) * (len(dims) - dim - 1))

    gain = one(*cuts[0])
    for cut in cuts[1:]:
        gain = gain * one(*cut)
    return gain


def routed_block(key, own, number, rows, number_of, top, bound, skew):
    order = jax.random.permutation(key, number_of)
    heavy_load, usual = portions_of(number_of, rows * top, bound, skew, True), portions_of(number_of, rows * top, bound, skew, False)
    places = jnp.arange(number_of)

    def named(sizes, turn):
        used = int((sizes > 0).sum())
        fixed = max(1, used // 4)
        moved = fixed + (places - fixed + turn * (used - fixed)) % max(1, number_of - fixed)
        return jnp.zeros((number_of,), jnp.int32).at[order[jnp.where(places < fixed, places, moved)]].set(jnp.asarray(sizes, jnp.int32))

    sizes = jnp.where(number % 4 == 0, named(heavy_load, number // 4), named(usual, number - number // 4 - 1))
    mixed = jax.random.permutation(jax.random.fold_in(own, 3), number_of)
    donor, taker = mixed[0:number_of // 2 * 2:2], mixed[1:number_of // 2 * 2:2]
    slack = jnp.minimum(sizes[donor] - 1, bound - sizes[taker]) // 2
    slack = jnp.where((donor == order[0]) | (taker == order[0]) | (sizes[taker] == 0), 0, jnp.maximum(slack, 0))
    moved = jax.random.randint(jax.random.fold_in(own, 4), (number_of // 2,), 0, 1 << 20) % (slack + 1)
    sizes = sizes.at[donor].add(-moved).at[taker].add(moved)
    members = jnp.searchsorted(jnp.cumsum(sizes), jnp.arange(rows * top), side="right").astype(jnp.int32)
    table = members.reshape(top, rows).T
    table = table[jax.random.permutation(jax.random.fold_in(own, 1), rows)]
    turn = jax.random.randint(jax.random.fold_in(own, 2), (rows, 1), 0, top)
    return jnp.take_along_axis(table, (jnp.arange(top)[None, :] + turn) % top, axis=1)


def portions_of(amount, total, most, lean, full):
    loads = [(1 << 20) // math.isqrt(standing ** lean) + 1 for standing in range(1, amount + 1)]
    largest = most if full else min(most, max(-(-total // amount), total * loads[0] // sum(loads)))
    least = 1 if total - largest >= amount - 1 else 0
    counts, spare = [largest] + [least] * (amount - 1), total - largest - least * (amount - 1)
    while spare > 0:
        movable = [i for i in range(1, amount) if counts[i] < largest] or [i for i in range(1, amount) if counts[i] < most]
        whole, left = sum([loads[i] for i in movable]), spare
        for i in movable:
            more = min(most - counts[i], max(1, left * loads[i] // whole), spare)
            counts[i] = counts[i] + more
            spare = spare - more
    return np.array(counts)


def normal_values(own_key, dims, width, reach, cuts=(), held_as=jnp.bfloat16):
    values = width * jax.random.normal(own_key, dims, jnp.float32)
    if cuts:
        values = values * level_of(own_key, dims, cuts, -0.22, 0.18)
    return jnp.clip(values, -reach, reach).astype(held_as)


def setup_inputs(seed: int = 0) -> dict:
    seeds = jax.random.split(jax.random.key(seed), 10)
    inputs = normal_values(seeds[0], (TOKENS, D), 1.0, 6.0, ((0, 32),))
    out_grad = normal_values(seeds[1], (TOKENS, D), 1.0, 6.0, ((0, 32),))
    routes_keys = jax.random.split(jax.random.fold_in(seeds[2], 1), TOKENS // TOK_DEV)
    routes_turns = jax.random.permutation(jax.random.fold_in(seeds[2], 3), TOKENS // TOK_DEV)
    routes = jax.vmap(lambda own, number: routed_block(jax.random.fold_in(seeds[2], 2), own, number, TOK_DEV, EXPERTS, TOP, CAP, 2))(routes_keys, routes_turns).reshape((TOKENS, TOP))
    combine = jnp.clip(jnp.exp(math.log(1.0) - 2.9957323 * jax.random.uniform(seeds[3], (TOKENS, TOP), jnp.float32) ** level_of(seeds[3], (TOKENS, TOP), ((0, 32),), -0.2, 0.2)), 0.05, 1.0)
    saved_gate = normal_values(seeds[4], (REPLICAS, EXPERTS, SLOTS, FF), 1.0, 6.0, ((0, 2), (1, 16)))
    saved_up = normal_values(seeds[5], (REPLICAS, EXPERTS, SLOTS, FF), 1.0, 6.0, ((0, 2), (1, 16)))
    w_gate = normal_values(seeds[6], (EXPERTS, D, FF), D ** -0.5, 0.125, ((0, 16), (1, 2)))
    w_up = normal_values(seeds[7], (EXPERTS, D, FF), D ** -0.5, 0.125, ((0, 16), (1, 2)))
    w_down = normal_values(seeds[8], (EXPERTS, FF, D), FF ** -0.5, 0.21875, ((0, 16), (2, 2)))
    return dict(inputs=inputs, out_grad=out_grad, routes=routes, combine=combine, saved_gate=saved_gate, saved_up=saved_up, w_gate=w_gate, w_up=w_up, w_down=w_down)


def slot_table(routes):
    blocks = TOKENS // TOK_DEV
    choices_flat = routes.reshape(blocks, TOK_DEV * TOP)
    expert_ids = jnp.arange(EXPERTS, dtype=jnp.int32)
    matches = (choices_flat[:, :, None] == expert_ids[None, None, :]).astype(jnp.int32)
    earlier = jnp.cumsum(matches, axis=1) - matches
    position = jnp.sum(earlier * matches, axis=2)
    block_ids = jnp.arange(blocks, dtype=jnp.int32)[:, None]
    replica = block_ids // EXPERTS
    sender = block_ids % EXPERTS
    slot_index = ((replica * EXPERTS + choices_flat) * SLOTS + sender * CAP + position).reshape(-1)
    return slot_index.astype(jnp.int32)


def reference(inputs, out_grad, routes, combine, saved_gate, saved_up, w_gate, w_up, w_down):
    count = TOKENS * TOP
    total = REPLICAS * EXPERTS * SLOTS
    slot_index = slot_table(routes)
    filler = jnp.full((total,), count, jnp.int32).at[slot_index].set(jnp.arange(count, dtype=jnp.int32))
    filler = filler.reshape(REPLICAS, EXPERTS, SLOTS).transpose(1, 0, 2)
    padded_in = jnp.concatenate([inputs, jnp.zeros((1, D), jnp.bfloat16)], axis=0)
    padded_out = jnp.concatenate([out_grad.astype(jnp.float32), jnp.zeros((1, D), jnp.float32)], axis=0)
    padded_mix = jnp.concatenate([combine.reshape(-1), jnp.zeros((1,), jnp.float32)], axis=0)

    def per_expert(index):
        source = filler[index]
        token_index = jnp.where(source < count, source // TOP, TOKENS).astype(jnp.int32)
        rows_in = padded_in[token_index]
        rows_out = (padded_mix[source][..., None] * padded_out[token_index]).astype(jnp.bfloat16)
        gate_pre = saved_gate[:, index].astype(jnp.float32)
        up_pre = saved_up[:, index].astype(jnp.float32)
        sigmoid_gate = jax.nn.sigmoid(gate_pre)
        silu_gate = gate_pre * sigmoid_gate
        hidden = (silu_gate * up_pre).astype(jnp.bfloat16)
        gate_mat = w_gate[index].astype(jnp.float32)
        up_mat = w_up[index].astype(jnp.float32)
        down_mat = w_down[index].astype(jnp.float32)
        grad_hidden = jnp.einsum("rsd,fd->rsf", rows_out.astype(jnp.float32), down_mat)
        grad_g = (grad_hidden * up_pre * sigmoid_gate * (1.0 + gate_pre * (1.0 - sigmoid_gate))).astype(jnp.bfloat16)
        grad_u = (grad_hidden * silu_gate).astype(jnp.bfloat16)
        rows_back = (jnp.einsum("rsf,df->rsd", grad_g.astype(jnp.float32), gate_mat)
                     + jnp.einsum("rsf,df->rsd", grad_u.astype(jnp.float32), up_mat)).astype(jnp.bfloat16)
        rows_in32 = rows_in.astype(jnp.float32)
        gate_part = jnp.einsum("rsd,rsf->df", rows_in32, grad_g.astype(jnp.float32))
        up_part = jnp.einsum("rsd,rsf->df", rows_in32, grad_u.astype(jnp.float32))
        down_part = jnp.einsum("rsf,rsd->fd", hidden.astype(jnp.float32), rows_out.astype(jnp.float32))
        return rows_back, gate_part, up_part, down_part

    rows_back, gate_grad, up_grad, down_grad = lax.map(per_expert, jnp.arange(EXPERTS, dtype=jnp.int32))
    table = rows_back.transpose(1, 0, 2, 3).reshape(total, D)
    places = slot_index.reshape(TOKENS, TOP)

    def accumulate(step, summed):
        column = lax.dynamic_index_in_dim(places, step, axis=1, keepdims=False)
        return summed + table[column].astype(jnp.float32)

    summed = lax.fori_loop(0, TOP, accumulate, jnp.zeros((TOKENS, D), jnp.float32))
    return summed.astype(jnp.bfloat16), gate_grad, up_grad, down_grad
```

```python
import functools

import jax
import jax.numpy as jnp
import numpy as np
from jax import lax
from jax.experimental import pallas as pl
from jax.experimental.pallas import tpu as pltpu
from jax.sharding import PartitionSpec as P


BOTH = ("dp", "expert")
ANY = pl.ANY


def line_ring(size):
    return [0] + list(range(1, size, 2)) + list(range(2, size, 2))[::-1]


def grid_of(experts):
    side = 1
    while (2 * side) ** 3 <= experts and experts % (4 * side * side) == 0:
        side *= 2
    return experts // (side * side), side, side


def places(experts, replicas):
    sizes = grid_of(experts)
    rings = [line_ring(size) for size in sizes]

    def coords(e):
        return [e // (sizes[1] * sizes[2]), (e // sizes[2]) % sizes[1], e % sizes[2]]

    def number(c):
        return (c[0] * sizes[1] + c[1]) * sizes[2] + c[2]

    def moved(e, axis, by):
        c = coords(e)
        ring = rings[axis]
        c[axis] = ring[(ring.index(c[axis]) + by) % len(ring)]
        return number(c)

    def axes(r):
        return (0, 2, 1) if r % 2 == 0 else (0, 1, 2)

    perms = [
        [
            (r * experts + e, r * experts + moved(e, axes(r)[which], 1))
            for r in range(replicas)
            for e in range(experts)
        ]
        for which in range(3)
    ]
    slow, side, _ = sizes
    table = np.zeros((replicas, experts, experts), np.int32)
    for r in range(replicas):
        _, early, late = axes(r)
        for e in range(experts):
            n = 0
            for k in range(slow):
                for l in range(side):
                    for j in range(side):
                        table[r, e, n] = moved(moved(moved(e, 0, -k), late, -l), early, -j)
                        n += 1
    return sizes, perms, table


def nt(a, b):
    return lax.dot_general(a, b, (((1,), (1,)), ((), ())), preferred_element_type=jnp.float32)


def tn(a, b):
    return lax.dot_general(a, b, (((0,), (0,)), ((), ())), preferred_element_type=jnp.float32)


def expert_kernel(blocks, cap, half, hid, *refs):
    refs = list(refs)
    idx, weight, pos = refs[:3]
    dys = refs[3 : 3 + blocks]
    rest = refs[3 + blocks :]
    wds, wgs, wus = rest[0:2], rest[2:4], rest[4:6]
    gate, up = rest[6:8]
    outs = rest[8 : 8 + blocks]
    pack, own_rows = rest[8 + blocks : 10 + blocks]
    (dyv, wdv, wgv, wuv, gv, uv, hot, packv, ownv, cv, in_sem, w_sem, s_sem, out_sem) = rest[10 + blocks :]
    tokens = dyv.shape[1]
    core = idx[0]
    offs = [pl.multiple_of(core * half, 128), pl.multiple_of((1 - core) * half, 128)]

    loads = [pltpu.make_async_copy(dys[b], dyv.at[b], in_sem.at[b]) for b in range(blocks)]
    wloads = []
    for n, (src, dst) in enumerate(((wds, wdv), (wgs, wgv), (wus, wuv))):
        wloads += [pltpu.make_async_copy(src[h], dst.at[h], w_sem.at[2 * n + h]) for h in range(2)]
    sloads = []
    for b in range(blocks):
        start = pl.multiple_of(idx[1 + b] * cap, 8)
        sloads.append(
            pltpu.make_async_copy(gate.at[pl.ds(start, cap)], gv.at[pl.ds(b * cap, cap)], s_sem.at[2 * b])
        )
        sloads.append(
            pltpu.make_async_copy(up.at[pl.ds(start, cap)], uv.at[pl.ds(b * cap, cap)], s_sem.at[2 * b + 1])
        )
    for c in loads + wloads[:2] + sloads + wloads[2:]:
        c.start()

    slots = lax.broadcasted_iota(jnp.int32, (cap, tokens), 0)
    for b in range(blocks):
        loads[b].wait()
        s = idx[1 + b]
        pick = slots == pos[pl.ds(s, 1), :]
        scale = jnp.sum(jnp.where(pick, weight[pl.ds(s, 1), :], 0.0), axis=1, keepdims=True)
        onehot = jnp.where(pick, 1.0, 0.0).astype(jnp.bfloat16)
        hot[b * cap : (b + 1) * cap, :] = onehot
        for h in range(2):
            rows = jnp.dot(onehot, dyv[b, :, pl.ds(offs[h], half)], preferred_element_type=jnp.float32)
            rows = (rows * scale).astype(jnp.bfloat16)
            if h == 0:
                ownv[b * cap : (b + 1) * cap, :] = rows
            else:
                packv[b * cap : (b + 1) * cap, 3 * hid :] = rows
    own_out = pltpu.make_async_copy(ownv, own_rows, out_sem.at[0])
    own_out.start()
    wloads[0].wait()
    wloads[1].wait()
    for c in sloads:
        c.wait()
    tile = 256
    for n in range(hid // tile):
        cols = pl.ds(n * tile, tile)
        gh = nt(ownv[...], wdv[0, cols, :]) + nt(packv[:, 3 * hid :], wdv[1, cols, :])
        g = gv[:, cols].astype(jnp.float32)
        u = uv[:, cols].astype(jnp.float32)
        sig = jax.nn.sigmoid(g)
        silu = g * sig
        packv[:, pl.ds(n * tile, tile)] = (gh * u * sig * (1.0 + g * (1.0 - sig))).astype(jnp.bfloat16)
        packv[:, pl.ds(hid + n * tile, tile)] = (gh * silu).astype(jnp.bfloat16)
        packv[:, pl.ds(2 * hid + n * tile, tile)] = (silu * u).astype(jnp.bfloat16)
    pack_out = pltpu.make_async_copy(packv, pack, out_sem.at[1])
    pack_out.start()
    for c in wloads[2:]:
        c.wait()
    for h in range(2):
        def body(n, carry):
            cols = pl.ds(pl.multiple_of(n * tile, tile), tile)
            back = nt(packv[:, 0:hid], wgv[h, cols, :]) + nt(packv[:, hid : 2 * hid], wuv[h, cols, :])
            back = back.astype(jnp.bfloat16)
            to = pl.ds(pl.multiple_of(offs[h] + n * tile, 128), tile)
            for b in range(blocks):
                part = tn(hot[b * cap : (b + 1) * cap, :], back[b * cap : (b + 1) * cap, :])
                cv[b, :, to] = part.astype(jnp.bfloat16)
            return carry

        lax.fori_loop(0, half // tile, body, 0)
    stores = [pltpu.make_async_copy(cv.at[b], outs[b], out_sem.at[2 + b]) for b in range(blocks)]
    for c in stores:
        c.start()
    own_out.wait()
    pack_out.wait()
    for c in stores:
        c.wait()


def run_expert(idx, weight, pos, dys, wds, wgs, wus, gate, up, cap):
    blocks = len(dys)
    tokens, width = dys[0].shape
    half = width // 2
    hid = gate.shape[1]
    rows = blocks * cap
    bf = jnp.bfloat16
    smem = pl.BlockSpec(memory_space=pltpu.SMEM)
    vmem = pl.BlockSpec(memory_space=pltpu.VMEM)
    hbm = pl.BlockSpec(memory_space=ANY)
    out = pl.pallas_call(
        functools.partial(expert_kernel, blocks, cap, half, hid),
        out_shape=[jax.ShapeDtypeStruct((tokens, width), bf)] * blocks
        + [jax.ShapeDtypeStruct((rows, 3 * hid + half), bf), jax.ShapeDtypeStruct((rows, half), bf)],
        in_specs=[smem, vmem, vmem] + [hbm] * (blocks + 8),
        out_specs=[hbm] * (blocks + 2),
        scratch_shapes=[
            pltpu.VMEM((blocks, tokens, width), bf),
            pltpu.VMEM((2, hid, half), bf),
            pltpu.VMEM((2, half, hid), bf),
            pltpu.VMEM((2, half, hid), bf),
            pltpu.VMEM((rows, hid), bf),
            pltpu.VMEM((rows, hid), bf),
            pltpu.VMEM((rows, tokens), bf),
            pltpu.VMEM((rows, 3 * hid + half), bf),
            pltpu.VMEM((rows, half), bf),
            pltpu.VMEM((blocks, tokens, width), bf),
            pltpu.SemaphoreType.DMA((blocks,)),
            pltpu.SemaphoreType.DMA((6,)),
            pltpu.SemaphoreType.DMA((2 * blocks,)),
            pltpu.SemaphoreType.DMA((2 + blocks,)),
        ],
        compiler_params=pltpu.CompilerParams(vmem_limit_bytes=48 << 20),
        cost_estimate=pl.CostEstimate(
            flops=2 * rows * width * hid * 3, bytes_accessed=20 << 20, transcendentals=rows * hid
        ),
        name="expert_rows",
    )(idx, weight, pos, *dys, *wds, *wgs, *wus, gate, up)
    return list(out[:blocks]), out[blocks], out[blocks + 1]


def pick_kernel(blocks, cap, swap, idx, pos, *refs):
    xs, (own, other) = refs[:blocks], refs[blocks:]
    tokens = xs[0].shape[0] // 2
    slots = lax.broadcasted_iota(jnp.int32, (cap, tokens), 0)
    for b in range(blocks):
        s = idx[1 + b]
        for r, to in ((0, own), (1, other)):
            at = b if r == 0 else swap[b]
            onehot = jnp.where(slots == pos[r, pl.ds(s, 1), :], 1.0, 0.0).astype(jnp.bfloat16)
            rows = jnp.dot(onehot, xs[b][r * tokens : (r + 1) * tokens, :], preferred_element_type=jnp.float32)
            to[at * cap : (at + 1) * cap, :] = rows.astype(jnp.bfloat16)


def run_pick(idx, pos, xs, cap, swap):
    blocks = len(xs)
    half = xs[0].shape[1]
    vmem = pl.BlockSpec(memory_space=pltpu.VMEM)
    shape = jax.ShapeDtypeStruct((blocks * cap, half), jnp.bfloat16)
    return pl.pallas_call(
        functools.partial(pick_kernel, blocks, cap, swap),
        out_shape=[shape, shape],
        in_specs=[pl.BlockSpec(memory_space=pltpu.SMEM)] + [vmem] * (1 + blocks),
        out_specs=[vmem, vmem],
        compiler_params=pltpu.CompilerParams(vmem_limit_bytes=32 << 20),
        cost_estimate=pl.CostEstimate(flops=1 << 28, bytes_accessed=8 << 20, transcendentals=0),
        name="pick_rows",
    )(idx, pos, *xs)


def down_kernel(count, *refs):
    hs, rs, out = refs[:count], refs[count : 2 * count], refs[2 * count]
    total = tn(hs[0][...], rs[0][...])
    for n in range(1, count):
        total += tn(hs[n][...], rs[n][...])
    out[...] = total


def run_down(packs, owns, others, hid, half):
    rows = packs[0].shape[0]
    tile = 256
    first = (3 * hid) // tile
    h_spec = pl.BlockSpec((rows, hid), lambda n: (0, 2))
    own_spec = pl.BlockSpec((rows, tile), lambda n: (0, n))
    other_spec = pl.BlockSpec((rows, tile), lambda n: (0, first + n))
    count = 2 * len(packs)
    return pl.pallas_call(
        functools.partial(down_kernel, count),
        grid=(half // tile,),
        out_shape=jax.ShapeDtypeStruct((hid, half), jnp.float32),
        in_specs=[h_spec] * count + [own_spec] * len(packs) + [other_spec] * len(packs),
        out_specs=pl.BlockSpec((hid, tile), lambda n: (0, n)),
        compiler_params=pltpu.CompilerParams(vmem_limit_bytes=40 << 20),
        cost_estimate=pl.CostEstimate(
            flops=2 * rows * count * hid * half, bytes_accessed=16 << 20, transcendentals=0
        ),
        name="down_grad",
    )(*packs, *others, *owns, *others)


def gate_up_kernel(count, *refs):
    xs, gs, us = refs[:count], refs[count : 2 * count], refs[2 * count : 3 * count]
    gate, up = refs[3 * count :]
    a = tn(xs[0][...], gs[0][...])
    for n in range(1, count):
        a += tn(xs[n][...], gs[n][...])
    gate[...] = a
    b = tn(xs[0][...], us[0][...])
    for n in range(1, count):
        b += tn(xs[n][...], us[n][...])
    up[...] = b


def run_gate_up(xs, packs, hid):
    rows, half = xs[0].shape
    tile = 256
    count = len(xs)
    x_spec = pl.BlockSpec((rows, tile), lambda m: (0, m))
    g_spec = pl.BlockSpec((rows, hid), lambda m: (0, 0))
    u_spec = pl.BlockSpec((rows, hid), lambda m: (0, 1))
    o_spec = pl.BlockSpec((tile, hid), lambda m: (m, 0))
    shape = jax.ShapeDtypeStruct((half, hid), jnp.float32)
    return pl.pallas_call(
        functools.partial(gate_up_kernel, count),
        grid=(half // tile,),
        out_shape=[shape, shape],
        in_specs=[x_spec] * count + [g_spec] * count + [u_spec] * count,
        out_specs=[o_spec, o_spec],
        compiler_params=pltpu.CompilerParams(vmem_limit_bytes=48 << 20),
        cost_estimate=pl.CostEstimate(
            flops=4 * rows * count * hid * half, bytes_accessed=24 << 20, transcendentals=0
        ),
        name="gate_up_grad",
    )(*xs, *packs, *packs)


def shards(inputs, out_grad, routes, combine, saved_gate, saved_up, w_gate, w_up, w_down):
    experts = lax.axis_size("expert")
    replicas = lax.axis_size("dp")
    tokens, width = inputs.shape
    half = width // replicas
    gate, up = saved_gate[0, 0], saved_up[0, 0]
    cap = gate.shape[0] // experts
    hid = gate.shape[1]
    (slow, side, _), perms, table = places(experts, replicas)
    core = lax.axis_index("dp")
    me = lax.axis_index("expert")
    bf = jnp.bfloat16
    swap_pairs = [(r, (r + 1) % replicas) for r in range(replicas)]
    swapped = [(b % side) * side + b // side for b in range(side * side)]

    def along(a, which):
        return lax.ppermute(a, BOTH, perms[which])

    def partner(a):
        return lax.ppermute(a, "dp", swap_pairs)

    order = jnp.asarray(table)[core, me]
    idx = [
        jnp.concatenate([core[None].astype(jnp.int32), order[k * side * side : (k + 1) * side * side]])
        for k in range(slow)
    ]

    ids = jnp.arange(experts, dtype=jnp.int32)
    routes_t, combine_t = routes.T, combine.T
    mine = jnp.sum(
        jnp.where(routes_t[None] == ids[:, None, None], combine_t[None], 0.0), axis=1
    )
    weight = lax.all_to_all(mine, "expert", split_axis=0, concat_axis=0, tiled=True)
    weights = jnp.stack([weight, partner(weight)])
    chosen = weights > 0
    before = jnp.arange(tokens)[:, None] < jnp.arange(tokens)[None, :]
    pos = lax.dot_general(
        chosen.astype(bf), before.astype(bf), (((2,), (0,)), ((), ())), preferred_element_type=jnp.float32
    )
    pos = jnp.where(chosen, pos.astype(jnp.int32), -1)

    wds = [w_down[0], partner(w_down[0])]
    wgs = [w_gate[0], partner(w_gate[0])]
    wus = [w_up[0], partner(w_up[0])]
    x_own = lax.dynamic_slice_in_dim(inputs, core * half, half, 1)
    x_away = lax.dynamic_slice_in_dim(inputs, (1 - core) * half, half, 1)
    x_half = jnp.concatenate([x_own, partner(x_away)], axis=0)

    keys = [(k, l, j) for k in range(slow) for l in range(side) for j in range(side)]
    gather_phases = slow + 2 * side - 3
    x_from = gather_phases - 1
    rs_from = x_from + gather_phases - 1
    rs_phases = slow + 2 * side - 3
    k_order = list(range(1, slow)) + [0]
    dy = {(0, 0, 0): out_grad}
    xg = {(0, 0, 0): x_half}
    contributions, packs, owns, others, picked = {}, {}, {}, {}, {}
    late_acc, early_acc, slow_acc = {}, {}, {}
    result = {}
    f32 = jnp.float32

    def source(key):
        k, l, j = key
        if l:
            return (k, l - 1, j), 2
        if j:
            return (k, 0, j - 1), 1
        return (k - 1, 0, 0), 0

    must = []
    for phase in range(rs_from + rs_phases):
        jobs = []
        for store, start in ((dy, 0), (xg, x_from)):
            for key in keys:
                if sum(key) and start + sum(key) - 1 == phase:
                    src, which = source(key)
                    jobs.append((store, key, store[src], which))
        for q, k in enumerate(k_order):
            t = phase - rs_from - q
            if 0 <= t < side - 1:
                for j in list(range(1, side)) + [0]:
                    a = contributions[k][(t + 1) * side + j]
                    if t:
                        a = (a.astype(f32) + late_acc[k, j].astype(f32)).astype(bf)
                    jobs.append((late_acc, (k, j), a, 2))
            t -= side - 1
            if 0 <= t < side - 1:
                j = t + 1
                a = contributions[k][j].astype(f32) + late_acc[k, j].astype(f32)
                if t:
                    a += early_acc[k].astype(f32)
                jobs.append((early_acc, k, a.astype(bf), 1))
            t -= side - 1
            if t == 0:
                a = contributions[k][0].astype(f32) + late_acc[k, 0].astype(f32) + early_acc[k].astype(f32)
                if q:
                    a += slow_acc[0].astype(f32)
                a = a.astype(bf)
                if k:
                    jobs.append((slow_acc, 0, a, 0))
                else:
                    result[0] = a
        sent = [job[2] for job in jobs]
        if phase:
            sent, must = lax.optimization_barrier((sent, must))
        got = [along(a, job[3]) for a, job in zip(sent, jobs)]
        for job, a in zip(jobs, got):
            job[0][job[1]] = a
        must = []
        k = phase - 2 * side + 2
        if 0 <= k < slow:
            mine_dy = [dy[k, l, j] for l in range(side) for j in range(side)]
            contributions[k], packs[k], owns[k] = run_expert(
                idx[k], weights[0], pos[0], mine_dy, wds, wgs, wus, gate, up, cap
            )
            others[k] = partner(packs[k])
            must += [packs[k]]
        if phase == 2 * side - 2 + slow + 1:
            down = run_down(
                [packs[k] for k in range(slow)],
                [owns[k] for k in range(slow)],
                [others[k] for k in range(slow)],
                hid,
                half,
            )
            must += [down]
        k = phase - x_from - 2 * side + 2
        if 0 <= k < slow:
            blocks = [xg[k, l, j] for l in range(side) for j in range(side)]
            picked[k] = run_pick(idx[k], pos, blocks, cap, swapped)
            must += [picked[k][0]]
        if k == slow:
            gate_grad, up_grad = run_gate_up(
                [picked[k][0] for k in range(slow)] + [picked[k][1] for k in range(slow)],
                [packs[k] for k in range(slow)] + [others[k] for k in range(slow)],
                hid,
            )
            must += [gate_grad, up_grad]
    last = k_order[-1]
    a = contributions[last][0].astype(f32) + late_acc[last, 0].astype(f32) + early_acc[last].astype(f32)
    input_grad = (a + slow_acc[0].astype(f32)).astype(bf)
    return (input_grad, gate_grad[None], up_grad[None], down[None])


def solution(mesh):
    return jax.shard_map(
        shards,
        mesh=mesh,
        in_specs=(
            P(("dp", "expert"), None),
            P(("dp", "expert"), None),
            P(("dp", "expert"), None),
            P(("dp", "expert"), None),
            P("dp", "expert", None, None),
            P("dp", "expert", None, None),
            P("expert", "dp", None),
            P("expert", "dp", None),
            P("expert", None, "dp"),
        ),
        out_specs=(
            P(("dp", "expert"), None),
            P("expert", "dp", None),
            P("expert", "dp", None),
            P("expert", None, "dp"),
        ),
        check_vma=False,
    )
```
